32 devices in a mesh: dp: 16 (over z, y, x), mp: 2 (over core).
Axes of the slice: x: 2, y: 2, z: 4, core: 2. Of those that a mesh axis runs over, the one named last changes fastest.
Arguments:
- new_embed: bfloat16 [1792, 1280], P('dp'), may hold values from -3 to 3
- context_key_cache: bfloat16 [1792, 16, 1280], P('dp', None, 'mp'), may hold values from -2500 to 2500
- value_cache: bfloat16 [1792, 16, 1280], P('dp', None, 'mp'), may hold values from -6 to 6
- valid: int32 [1792], P('dp'), may hold values from 2 to 16
- attn_gain: float32 [1280], replicated, may hold values from 0.1 to 1.9
- mlp_gain: float32 [1280], replicated, may hold values from 0.1 to 1.9
- query_scale: float32 [80], replicated, may hold values from 0.1 to 1.9
- w_qkv: bfloat16 [3, 1280, 1280], P(None, 'dp', 'mp'), may hold values from -0.15625 to 0.15625
- w_out: bfloat16 [1280, 1280], P('mp', 'dp'), may hold values from -0.625 to 0.625
- w_up: bfloat16 [1280, 1280], P('dp', 'mp'), may hold values from -0.15625 to 0.15625
- w_down: bfloat16 [1280, 1280], P('mp', 'dp'), may hold values from -0.15625 to 0.15625
- head_hidden: bfloat16 [1280, 1280], P('dp', 'mp'), may hold values from -0.15625 to 0.15625
- final_layer_matrices: bfloat16 [2, 1280, 1280], P(None, 'mp', 'dp'), may hold values from -0.15625 to 0.15625
Outputs:
- predicted_levels: float32 [1792, 1280], P('dp', 'mp')
The draws below stay inside these ranges and needn't reach their ends.
Inputs may be any that keep to these rules, and one draw needn't show every extreme that they name: Series s uses its first valid[s] cached patches.
All inputs are finite; a program needn't handle non-finite values.
Results may differ from the reference program's by a relative error of at most 0.035.
Values may be sent and summed in bfloat16 or wider, within the bound.
A program may use at most 128 MiB of HBM per device.

```python
import math
import jax
import jax.numpy as jnp
from jax import lax

D = 1280
FF = 1280
HEADS = 16
OUT = 1280
SER_DEV = 112
CTX = 16
HD = 80
SERIES = 1792
N_DP = 16


def draw_context_key_cache(key, part):
    base = jnp.clip(jax.random.normal(key, (SERIES, CTX, D), jnp.float32), -6.0, 6.0)
    result = base
    return result.astype(jnp.bfloat16)


def touch_ends(values, stream_key, least, high):
    index_at = [jax.random.randint(jax.random.fold_in(stream_key, axis), (), 0, length) for axis, length in enumerate(values.shape)]
    main_axis = values.shape.index(max(values.shape))
    beside = index_at[:main_axis] + [(index_at[main_axis] + 1) % values.shape[main_axis]] + index_at[main_axis + 1:]
    return values.at[tuple(index_at)].set(least).at[tuple(beside)].set(high)


def block_scale(key, shape, cuts, low, largest):
    def one(position, blocks):
        draws = jax.random.uniform(jax.random.fold_in(jax.random.fold_in(key, 6), position), (blocks,), jnp.float32, low / len(cuts), largest / len(cuts))
        return jnp.repeat(jnp.exp(draws), shape[position] // blocks).reshape((-1,) + (1,) * (len(shape) - position - 1))

    level = one(*cuts[0])
    for cut in cuts[1:]:
        level = level * one(*cut)
    return level


def centred(rng, dims, scale, limit, pieces=(), kind=jnp.bfloat16):
    values = scale * jax.random.normal(rng, dims, jnp.float32)
    if pieces:
        values = values * block_scale(rng, dims, pieces, -0.22, 0.18)
    return jnp.clip(values, -limit, limit).astype(kind)


def setup_inputs(seed: int = 0) -> dict:
    arg_keys = jax.random.split(jax.random.key(seed), 14)
    new_embed = centred(arg_keys[0], (SERIES, D), 0.5, 3.0, ((0, 16),))
    context_key_cache = draw_context_key_cache(jax.random.fold_in(arg_keys[13], 71), 0)
    value_cache = centred(arg_keys[2], (SERIES, CTX, D), 1.0, 6.0, ((0, 16), (2, 2)))
    valid = touch_ends(jax.random.randint(arg_keys[3], (SERIES,), 2, CTX + 1), jax.random.fold_in(arg_keys[3], 1), 2, CTX).astype(jnp.int32)
    attn_gain = jnp.clip(1.0 + 0.18 * jax.random.normal(arg_keys[4], (D,), jnp.float32), 0.1, 1.9)
    mlp_gain = jnp.clip(1.0 + 0.18 * jax.random.normal(arg_keys[5], (D,), jnp.float32), 0.1, 1.9)
    query_scale = jnp.clip(1.0 + 0.18 * jax.random.normal(arg_keys[6], (HD,), jnp.float32), 0.1, 1.9)
    w_qkv = centred(arg_keys[7], (3, D, D), D ** -0.5, 0.15625, ((1, 16), (2, 2)))
    w_out = centred(arg_keys[8], (D, D), (D // 16) ** -0.5, 0.625, ((0, 2), (1, 16)))
    w_up = centred(arg_keys[9], (D, FF), D ** -0.5, 0.15625, ((0, 16), (1, 2)))
    w_down = centred(arg_keys[10], (FF, D), FF ** -0.5, 0.15625, ((0, 2), (1, 16)))
    head_hidden = centred(arg_keys[11], (D, D), D ** -0.5, 0.15625, ((0, 16), (1, 2)))
    final_layer_matrices = centred(arg_keys[12], (2, D, OUT), D ** -0.5, 0.15625, ((1, 2), (2, 16)))
    return dict(new_embed=new_embed, context_key_cache=context_key_cache, value_cache=value_cache, valid=valid, attn_gain=attn_gain, mlp_gain=mlp_gain, query_scale=query_scale, w_qkv=w_qkv, w_out=w_out, w_up=w_up, w_down=w_down, head_hidden=head_hidden, final_layer_matrices=final_layer_matrices)


def rms_scale(values, gain):
    meansq = lax.optimization_barrier(jnp.mean(values * values, axis=-1, keepdims=True))
    return values * lax.rsqrt(meansq + 1e-06) * gain.astype(jnp.float32)

def attend(query_all, key_new, value_new, context_key_cache, value_cache, valid):
    count = context_key_cache.shape[0]
    context_len = context_key_cache.shape[1]
    cache_keys = context_key_cache.reshape(count, context_len, HEADS, HD).astype(jnp.float32)
    cache_vals = value_cache.reshape(count, context_len, HEADS, HD).astype(jnp.float32)
    query_full = query_all.astype(jnp.float32)
    scores = jnp.einsum('bhe,bche->bhc', query_full, cache_keys)
    own_score = lax.optimization_barrier(jnp.sum(query_full * key_new.astype(jnp.float32), axis=-1))
    in_use = jnp.arange(context_len, dtype=jnp.int32)[None, :] < valid[:, None]
    scores = jnp.where(in_use[:, None, :], scores, -jnp.inf)
    highest = jnp.maximum(lax.optimization_barrier(jnp.max(scores, axis=-1)), own_score)
    exp_cache = jnp.exp(scores - highest[..., None])
    exp_own = jnp.exp(own_score - highest)
    denominator = lax.optimization_barrier(jnp.sum(exp_cache, axis=-1)) + exp_own
    weight_cache = (exp_cache / denominator[..., None]).astype(jnp.bfloat16)
    weight_own = (exp_own / denominator).astype(jnp.bfloat16)
    context = jnp.einsum('bhc,bche->bhe', weight_cache.astype(jnp.float32), cache_vals)
    context = context + weight_own.astype(jnp.float32)[..., None] * value_new.astype(jnp.float32)
    return context.astype(jnp.bfloat16).reshape(count, D)

def reference(new_embed, context_key_cache, value_cache, valid, attn_gain, mlp_gain, query_scale, w_qkv, w_out, w_up, w_down, head_hidden, final_layer_matrices):
    stream = new_embed.astype(jnp.float32)
    normed = rms_scale(stream, attn_gain).astype(jnp.bfloat16)
    query_all = jnp.dot(normed, w_qkv[0], preferred_element_type=jnp.float32).reshape(SERIES, HEADS, HD)
    query_all = (query_all * query_scale.astype(jnp.float32) / math.sqrt(HD)).astype(jnp.bfloat16)
    key_new = jnp.dot(normed, w_qkv[1], preferred_element_type=jnp.float32).astype(jnp.bfloat16).reshape(SERIES, HEADS, HD)
    value_new = jnp.dot(normed, w_qkv[2], preferred_element_type=jnp.float32).astype(jnp.bfloat16).reshape(SERIES, HEADS, HD)
    blocked = (query_all.reshape(N_DP, SER_DEV, HEADS, HD), key_new.reshape(N_DP, SER_DEV, HEADS, HD), value_new.reshape(N_DP, SER_DEV, HEADS, HD), context_key_cache.reshape(N_DP, SER_DEV, CTX, D), value_cache.reshape(N_DP, SER_DEV, CTX, D), valid.reshape(N_DP, SER_DEV))
    context = lax.map(lambda items: attend(*items), blocked).reshape(SERIES, D)
    stream1 = stream + jnp.dot(context, w_out, preferred_element_type=jnp.float32)
    normed2 = rms_scale(stream1, mlp_gain).astype(jnp.bfloat16)
    hidden = jax.nn.relu(jnp.dot(normed2, w_up, preferred_element_type=jnp.float32)).astype(jnp.bfloat16)
    carried_signal_second = (stream1 + jnp.dot(hidden, w_down, preferred_element_type=jnp.float32)).astype(jnp.bfloat16)
    quantile_layer_nonlinear = jax.nn.silu(jnp.dot(carried_signal_second, head_hidden, preferred_element_type=jnp.float32)).astype(jnp.bfloat16)
    predicted_levels = jnp.dot(quantile_layer_nonlinear, final_layer_matrices[0], preferred_element_type=jnp.float32)
    predicted_levels = predicted_levels + jnp.dot(carried_signal_second, final_layer_matrices[1], preferred_element_type=jnp.float32)
    return predicted_levels
```

```python
import functools
import math

import jax
import jax.numpy as jnp
from jax import lax
from jax.experimental import pallas as pl
from jax.experimental.pallas import tpu as pltpu
from jax.sharding import PartitionSpec as P

MESH = pl.DeviceIdType.MESH


def grid_of(mesh):
    count = mesh.shape["dp"]
    try:
        coords = [tuple(d.coords) for d in mesh.devices[:, 0]]
        sizes = [len({c[k] for c in coords}) for k in (2, 1, 0)]
    except Exception:
        sizes = [count, 1, 1]
    if math.prod(sizes) != count:
        sizes = [count, 1, 1]
    return tuple(sizes)


def axis_orders(count):
    pattern = ((0, 1, 2), (0, 2, 1), (2, 1, 0), (0, 1, 2), (0, 2, 1), (0, 1, 2), (2, 1, 0), (0, 2, 1), (0, 1, 2))
    return [pattern[i % len(pattern)] for i in range(count)]


def gather_kernel(sizes, orders, own_ref, full_ref, local_sem, send_sem, recv_sem):
    me = lax.axis_index("dp")
    spans = (sizes[1] * sizes[2], sizes[2], 1)
    pos = tuple((me // spans[k]) % sizes[k] for k in range(3))

    def peer(axis, step):
        other = lax.rem(pos[axis] + step, sizes[axis])
        return me + (other - pos[axis]) * spans[axis]

    barrier = pltpu.get_barrier_semaphore()
    peers = [(axis, step) for axis in range(3) for step in range(1, sizes[axis])]
    for axis, step in peers:
        pl.semaphore_signal(barrier, inc=1, device_id={"dp": peer(axis, step)}, device_id_type=MESH)
    pl.semaphore_wait(barrier, len(peers))

    slot = {key: i for i, key in enumerate(peers)}

    def copies(m, phase):
        axis = orders[m][phase]
        done = orders[m][:phase]
        where = tuple(slice(None) if k in done else pos[k] for k in range(3))
        target = full_ref.at[(m,) + where]
        source = own_ref.at[m] if phase == 0 else target
        return [
            pltpu.make_async_remote_copy(
                src_ref=source,
                dst_ref=target,
                send_sem=send_sem.at[m, slot[axis, step]],
                recv_sem=recv_sem.at[m, slot[axis, step]],
                device_id={"dp": peer(axis, step)},
                device_id_type=MESH,
            )
            for step in range(1, sizes[axis])
        ]

    count = len(orders)
    flying = []
    local = []
    for m in range(count):
        flying.append(copies(m, 0))
        for copy in flying[m]:
            copy.start()
    for m in range(count):
        copy = pltpu.make_async_copy(own_ref.at[m], full_ref.at[(m,) + pos], local_sem.at[m])
        copy.start()
        local.append(copy)
    sent = []
    for phase in range(1, 3):
        for m in range(count):
            if phase == 1:
                local[m].wait()
            for copy in flying[m]:
                copy.wait_recv()
            sent += flying[m]
            flying[m] = copies(m, phase)
            for copy in flying[m]:
                copy.start()
    for m in range(count):
        for copy in flying[m]:
            copy.wait_recv()
        sent += flying[m]
    for copy in sent:
        copy.wait_send()


def gather_all(own, sizes):
    count, rows, columns = own.shape
    if rows % 16:
        return lax.all_gather(own, "dp", axis=1, tiled=True)
    slots = sum(size - 1 for size in sizes)
    full = pl.pallas_call(
        functools.partial(gather_kernel, sizes, axis_orders(count)),
        out_shape=jax.ShapeDtypeStruct((count,) + sizes + (rows, columns), own.dtype),
        in_specs=[pl.BlockSpec(memory_space=pltpu.VMEM)],
        out_specs=pl.BlockSpec(memory_space=pl.ANY),
        scratch_shapes=[
            pltpu.SemaphoreType.DMA((count,)),
            pltpu.SemaphoreType.DMA((count, slots)),
            pltpu.SemaphoreType.DMA((count, slots)),
        ],
        compiler_params=pltpu.CompilerParams(collective_id=0, has_side_effects=True),
        name="gather_weights",
    )(own)
    return full.reshape(count, math.prod(sizes) * rows, columns)


def swap(values):
    return lax.ppermute(values, "mp", [(0, 1), (1, 0)])


def rms_scale(values, gain):
    meansq = jnp.mean(values * values, axis=-1, keepdims=True)
    return values * lax.rsqrt(meansq + 1e-06) * gain


def dot_t(left, right):
    return lax.dot_general(
        left, right, (((1,), (1,)), ((), ())), preferred_element_type=jnp.float32
    )


def per_device(
    sizes,
    new_embed,
    context_key_cache,
    value_cache,
    valid,
    attn_gain,
    mlp_gain,
    query_scale,
    w_qkv,
    w_out,
    w_up,
    w_down,
    head_hidden,
    final_layer_matrices,
):
    row_count = new_embed.shape[0]
    context_len = context_key_cache.shape[1]
    local_width = context_key_cache.shape[2]
    head_size = query_scale.shape[0]
    local_heads = local_width // head_size
    mp_index = lax.axis_index("mp")
    own = jnp.concatenate(
        [
            w_qkv,
            w_out.T[None],
            w_up[None],
            w_down.T[None],
            head_hidden[None],
            jnp.swapaxes(final_layer_matrices, 1, 2),
        ],
        axis=0,
    )
    full = gather_all(own, sizes)
    stream = new_embed.astype(jnp.float32)
    normed = rms_scale(stream, attn_gain).astype(jnp.bfloat16)
    projected = [jnp.dot(normed, full[j], preferred_element_type=jnp.float32) for j in range(3)]
    query_all = projected[0].reshape(row_count, local_heads, head_size)
    query_all = (query_all * query_scale / math.sqrt(head_size)).astype(jnp.bfloat16)
    key_new = projected[1].astype(jnp.bfloat16).reshape(row_count, local_heads, head_size)
    value_new = projected[2].astype(jnp.bfloat16).reshape(row_count, local_heads, head_size)
    cache_keys = context_key_cache.reshape(row_count, context_len, local_heads, head_size)
    cache_vals = value_cache.reshape(row_count, context_len, local_heads, head_size)
    scores = jnp.einsum("bhe,bche->bhc", query_all, cache_keys, preferred_element_type=jnp.float32)
    own_score = jnp.sum(query_all.astype(jnp.float32) * key_new.astype(jnp.float32), axis=-1)
    in_use = jnp.arange(context_len, dtype=jnp.int32)[None, :] < valid[:, None]
    scores = jnp.where(in_use[:, None, :], scores, -jnp.inf)
    highest = jnp.maximum(jnp.max(scores, axis=-1), own_score)
    exp_cache = jnp.exp(scores - highest[..., None])
    exp_own = jnp.exp(own_score - highest)
    denominator = jnp.sum(exp_cache, axis=-1) + exp_own
    weight_cache = (exp_cache / denominator[..., None]).astype(jnp.bfloat16)
    weight_own = (exp_own / denominator).astype(jnp.bfloat16)
    context = jnp.einsum(
        "bhc,bche->bhe", weight_cache, cache_vals, preferred_element_type=jnp.float32
    )
    context = context + weight_own.astype(jnp.float32)[..., None] * value_new.astype(jnp.float32)
    context = context.astype(jnp.bfloat16).reshape(row_count, local_width)
    attention = dot_t(context, full[3]).astype(jnp.bfloat16)
    stream1 = stream + (attention.astype(jnp.float32) + swap(attention).astype(jnp.float32))
    normed2 = rms_scale(stream1, mlp_gain).astype(jnp.bfloat16)
    up_act = jnp.dot(normed2, full[4], preferred_element_type=jnp.float32)
    hidden = jax.nn.relu(up_act).astype(jnp.bfloat16)
    feed_out = dot_t(hidden, full[5]).astype(jnp.bfloat16)
    stream2 = stream1 + (feed_out.astype(jnp.float32) + swap(feed_out).astype(jnp.float32))
    stream2 = stream2.astype(jnp.bfloat16)
    half = final_layer_matrices.shape[1]
    stream_half = lax.dynamic_slice_in_dim(stream2, mp_index * half, half, 1)
    head_pre = jnp.dot(stream2, full[6], preferred_element_type=jnp.float32)
    head_act = jax.nn.silu(head_pre).astype(jnp.bfloat16)
    partial_out = dot_t(head_act, full[7]) + dot_t(stream_half, full[8])
    out_half = partial_out.shape[1] // 2
    mine = lax.dynamic_slice_in_dim(partial_out, mp_index * out_half, out_half, 1)
    theirs = lax.dynamic_slice_in_dim(partial_out, (1 - mp_index) * out_half, out_half, 1)
    return mine + swap(theirs.astype(jnp.bfloat16)).astype(jnp.float32)


def solution(mesh):
    in_specs = (
        P("dp", None),
        P("dp", None, "mp"),
        P("dp", None, "mp"),
        P("dp"),
        P(),
        P(),
        P(),
        P(None, "dp", "mp"),
        P("mp", "dp"),
        P("dp", "mp"),
        P("mp", "dp"),
        P("dp", "mp"),
        P(None, "mp", "dp"),
    )
    out_specs = P("dp", "mp")
    return jax.shard_map(
        functools.partial(per_device, grid_of(mesh)),
        mesh=mesh,
        in_specs=in_specs,
        out_specs=out_specs,
        check_vma=False,
    )
```

```python
import functools
import math

import jax
import jax.numpy as jnp
from jax import lax
from jax.experimental import pallas as pl
from jax.experimental.pallas import tpu as pltpu
from jax.sharding import PartitionSpec as P

MESH = pl.DeviceIdType.MESH


def grid_of(mesh):
    count = mesh.shape["dp"]
    try:
        coords = [tuple(d.coords) for d in mesh.devices[:, 0]]
        sizes = [len({c[k] for c in coords}) for k in (2, 1, 0)]
    except Exception:
        sizes = [count, 1, 1]
    if math.prod(sizes) != count:
        sizes = [count, 1, 1]
    return tuple(sizes)


def axis_orders(count):
    pair = ((0, 1, 2), (0, 2, 1))
    return [pair[m % 2] for m in range(count - 1)] + [(2, 1, 0)]


def gather_kernel(sizes, orders, own_counts, *refs):
    own_refs = refs[: len(own_counts)]
    full_ref, local_sem, send_sem, recv_sem = refs[len(own_counts) :]
    blocks = [ref.at[i] for ref, n in zip(own_refs, own_counts) for i in range(n)]
    me = lax.axis_index("dp")
    spans = (sizes[1] * sizes[2], sizes[2], 1)
    pos = tuple((me // spans[k]) % sizes[k] for k in range(3))

    def peer(axis, step):
        other = lax.rem(pos[axis] + step, sizes[axis])
        return me + (other - pos[axis]) * spans[axis]

    barrier = pltpu.get_barrier_semaphore()
    peers = [(axis, step) for axis in range(3) for step in range(1, sizes[axis])]
    for axis, step in peers:
        pl.semaphore_signal(barrier, inc=1, device_id={"dp": peer(axis, step)}, device_id_type=MESH)
    pl.semaphore_wait(barrier, len(peers))

    slot = {key: i for i, key in enumerate(peers)}

    def copies(m, phase):
        axis = orders[m][phase]
        done = orders[m][:phase]
        where = tuple(slice(None) if k in done else pos[k] for k in range(3))
        target = full_ref.at[(m,) + where]
        source = blocks[m] if phase == 0 else target
        return [
            pltpu.make_async_remote_copy(
                src_ref=source,
                dst_ref=target,
                send_sem=send_sem.at[m, slot[axis, step]],
                recv_sem=recv_sem.at[m, slot[axis, step]],
                device_id={"dp": peer(axis, step)},
                device_id_type=MESH,
            )
            for step in range(1, sizes[axis])
        ]

    count = len(orders)
    flying = [None] * count
    sent = []

    def begin(m, phase):
        if phase:
            for copy in flying[m]:
                copy.wait_recv()
            sent.extend(flying[m])
        flying[m] = copies(m, phase)
        for copy in flying[m]:
            copy.start()

    for m in [0, count - 1] + list(range(1, count - 1)):
        begin(m, 0)
    local = []
    for m in range(count):
        copy = pltpu.make_async_copy(blocks[m], full_ref.at[(m,) + pos], local_sem.at[m])
        copy.start()
        local.append(copy)
    for copy in local:
        copy.wait()
    begin(count - 1, 1)
    begin(count - 1, 2)
    for m in range(count):
        if m < count - 1:
            begin(m, 1)
        if m >= 1:
            begin(m - 1, 2)
    for m in range(count):
        for copy in flying[m]:
            copy.wait_recv()
        sent.extend(flying[m])
    for copy in sent:
        copy.wait_send()


def gather_all(owns, sizes):
    rows, columns = owns[0].shape[1:]
    counts = [own.shape[0] for own in owns]
    count = sum(counts)
    if rows % 16:
        return lax.all_gather(jnp.concatenate(owns, axis=0), "dp", axis=1, tiled=True)
    slots = sum(size - 1 for size in sizes)
    full = pl.pallas_call(
        functools.partial(gather_kernel, sizes, axis_orders(count), counts),
        out_shape=jax.ShapeDtypeStruct((count,) + sizes + (rows, columns), owns[0].dtype),
        in_specs=[pl.BlockSpec(memory_space=pltpu.VMEM)] * len(owns),
        out_specs=pl.BlockSpec(memory_space=pl.ANY),
        scratch_shapes=[
            pltpu.SemaphoreType.DMA((count,)),
            pltpu.SemaphoreType.DMA((count, slots)),
            pltpu.SemaphoreType.DMA((count, slots)),
        ],
        compiler_params=pltpu.CompilerParams(collective_id=0, has_side_effects=True),
        name="gather_weights",
    )(*owns)
    return full.reshape(count, math.prod(sizes) * rows, columns)


def swap(values):
    return lax.ppermute(values, "mp", [(0, 1), (1, 0)])


def rms_scale(values, gain):
    meansq = jnp.mean(values * values, axis=-1, keepdims=True)
    return values * lax.rsqrt(meansq + 1e-06) * gain


def dot_t(left, right):
    return lax.dot_general(
        left, right, (((1,), (1,)), ((), ())), preferred_element_type=jnp.float32
    )


def per_device(
    sizes,
    new_embed,
    context_key_cache,
    value_cache,
    valid,
    attn_gain,
    mlp_gain,
    query_scale,
    w_qkv,
    w_out,
    w_up,
    w_down,
    head_hidden,
    final_layer_matrices,
):
    row_count = new_embed.shape[0]
    context_len = context_key_cache.shape[1]
    local_width = context_key_cache.shape[2]
    head_size = query_scale.shape[0]
    local_heads = local_width // head_size
    mp_index = lax.axis_index("mp")
    owns = [
        w_qkv,
        w_out.T[None],
        w_up[None],
        w_down.T[None],
        head_hidden[None],
        jnp.swapaxes(final_layer_matrices, 1, 2),
    ]
    full = gather_all(owns, sizes)
    stream = new_embed.astype(jnp.float32)
    normed = rms_scale(stream, attn_gain).astype(jnp.bfloat16)
    projected = [jnp.dot(normed, full[j], preferred_element_type=jnp.float32) for j in range(3)]
    query_all = projected[0].reshape(row_count, local_heads, head_size)
    query_all = (query_all * query_scale / math.sqrt(head_size)).astype(jnp.bfloat16)
    key_new = projected[1].astype(jnp.bfloat16).reshape(row_count, local_heads, head_size)
    value_new = projected[2].astype(jnp.bfloat16).reshape(row_count, local_heads, head_size)
    cache_keys = context_key_cache.reshape(row_count, context_len, local_heads, head_size)
    cache_vals = value_cache.reshape(row_count, context_len, local_heads, head_size)
    scores = jnp.einsum("bhe,bche->bhc", query_all, cache_keys, preferred_element_type=jnp.float32)
    own_score = jnp.sum(query_all.astype(jnp.float32) * key_new.astype(jnp.float32), axis=-1)
    in_use = jnp.arange(context_len, dtype=jnp.int32)[None, :] < valid[:, None]
    scores = jnp.where(in_use[:, None, :], scores, -jnp.inf)
    highest = jnp.maximum(jnp.max(scores, axis=-1), own_score)
    exp_cache = jnp.exp(scores - highest[..., None])
    exp_own = jnp.exp(own_score - highest)
    denominator = jnp.sum(exp_cache, axis=-1) + exp_own
    weight_cache = (exp_cache / denominator[..., None]).astype(jnp.bfloat16)
    weight_own = (exp_own / denominator).astype(jnp.bfloat16)
    context = jnp.einsum(
        "bhc,bche->bhe", weight_cache, cache_vals, preferred_element_type=jnp.float32
    )
    context = context + weight_own.astype(jnp.float32)[..., None] * value_new.astype(jnp.float32)
    context = context.astype(jnp.bfloat16).reshape(row_count, local_width)
    attention = dot_t(context, full[3]).astype(jnp.bfloat16)
    stream1 = stream + (attention.astype(jnp.float32) + swap(attention).astype(jnp.float32))
    normed2 = rms_scale(stream1, mlp_gain).astype(jnp.bfloat16)
    up_act = jnp.dot(normed2, full[4], preferred_element_type=jnp.float32)
    hidden = jax.nn.relu(up_act).astype(jnp.bfloat16)
    feed_out = dot_t(hidden, full[5]).astype(jnp.bfloat16)
    stream2 = stream1 + (feed_out.astype(jnp.float32) + swap(feed_out).astype(jnp.float32))
    stream2 = stream2.astype(jnp.bfloat16)
    half = final_layer_matrices.shape[1]
    stream_half = lax.dynamic_slice_in_dim(stream2, mp_index * half, half, 1)
    head_pre = jnp.dot(stream2, full[6], preferred_element_type=jnp.float32)
    head_act = jax.nn.silu(head_pre).astype(jnp.bfloat16)
    partial_out = dot_t(head_act, full[7]) + dot_t(stream_half, full[8])
    out_half = partial_out.shape[1] // 2
    mine = lax.dynamic_slice_in_dim(partial_out, mp_index * out_half, out_half, 1)
    theirs = lax.dynamic_slice_in_dim(partial_out, (1 - mp_index) * out_half, out_half, 1)
    return mine + swap(theirs.astype(jnp.bfloat16)).astype(jnp.float32)


def solution(mesh):
    in_specs = (
        P("dp", None),
        P("dp", None, "mp"),
        P("dp", None, "mp"),
        P("dp"),
        P(),
        P(),
        P(),
        P(None, "dp", "mp"),
        P("mp", "dp"),
        P("dp", "mp"),
        P("mp", "dp"),
        P("dp", "mp"),
        P(None, "mp", "dp"),
    )
    out_specs = P("dp", "mp")
    return jax.shard_map(
        functools.partial(per_device, grid_of(mesh)),
        mesh=mesh,
        in_specs=in_specs,
        out_specs=out_specs,
        check_vma=False,
    )
```

```python
import functools
import math

import jax
import jax.numpy as jnp
from jax import lax
from jax.experimental import pallas as pl
from jax.experimental.pallas import tpu as pltpu
from jax.sharding import PartitionSpec as P

MESH = pl.DeviceIdType.MESH


def grid_of(mesh):
    count = mesh.shape["dp"]
    try:
        coords = [tuple(d.coords) for d in mesh.devices[:, 0]]
        sizes = [len({c[k] for c in coords}) for k in (2, 1, 0)]
    except Exception:
        sizes = [count, 1, 1]
    if math.prod(sizes) != count:
        sizes = [count, 1, 1]
    return tuple(sizes)


def axis_orders(count):
    pair = ((0, 1, 2), (0, 2, 1))
    return [pair[m % 2] for m in range(count - 1)] + [(2, 1, 0)]


def block_kernel(
    sizes,
    head_size,
    x_ref,
    key_ref,
    value_ref,
    valid_ref,
    attn_gain_ref,
    mlp_gain_ref,
    scale_ref,
    spread_ref,
    heads_ref,
    w_qkv_ref,
    w_out_ref,
    w_up_ref,
    w_down_ref,
    head_ref,
    final_ref,
    out_ref,
    full_ref,
    key_buf,
    value_buf,
    query_buf,
    fresh_buf,
    context_buf,
    swap_out,
    swap_in,
    half_bf,
    half_f32,
    part_bf,
    part_in,
    cache_sem,
    local_sem,
    send_sem,
    recv_sem,
    swap_send,
    swap_recv,
):
    own = [w_qkv_ref.at[j] for j in range(3)]
    own += [w_out_ref, w_up_ref, w_down_ref, head_ref, final_ref.at[0], final_ref.at[1]]
    count = len(own)
    orders = axis_orders(count)
    me = lax.axis_index("dp")
    mp = lax.axis_index("mp")
    spans = (sizes[1] * sizes[2], sizes[2], 1)
    pos = tuple((me // spans[k]) % sizes[k] for k in range(3))

    def peer(axis, step):
        other = lax.rem(pos[axis] + step, sizes[axis])
        return me + (other - pos[axis]) * spans[axis]

    cache_copies = [
        pltpu.make_async_copy(key_ref, key_buf, cache_sem.at[0]),
        pltpu.make_async_copy(value_ref, value_buf, cache_sem.at[1]),
    ]
    barrier = pltpu.get_barrier_semaphore()
    peers = [(axis, step) for axis in range(3) for step in range(1, sizes[axis])]
    for axis, step in peers:
        pl.semaphore_signal(barrier, inc=1, device_id={"dp": peer(axis, step)}, device_id_type=MESH)
    pl.semaphore_signal(barrier, inc=1, device_id={"mp": 1 - mp}, device_id_type=MESH)
    pl.semaphore_wait(barrier, len(peers) + 1)
    slot = {key: i for i, key in enumerate(peers)}

    def copies(m, phase):
        axis = orders[m][phase]
        done = orders[m][:phase]
        target = full_ref.at[(m,) + tuple(slice(None) if k in done else pos[k] for k in range(3))]
        return [
            pltpu.make_async_remote_copy(
                src_ref=target if phase else own[m],
                dst_ref=target,
                send_sem=send_sem.at[m, slot[axis, step]],
                recv_sem=recv_sem.at[m, slot[axis, step]],
                device_id={"dp": peer(axis, step)},
                device_id_type=MESH,
            )
            for step in range(1, sizes[axis])
        ]

    flying = [None] * count
    sent = []

    def arrive(m):
        for copy in flying[m]:
            copy.wait_recv()
        sent.extend(flying[m])

    def begin(m, phase):
        if phase:
            arrive(m)
        flying[m] = copies(m, phase)
        for copy in flying[m]:
            copy.start()

    ahead = 3
    for m in [0, count - 1] + list(range(1, ahead)):
        begin(m, 0)
    local = []
    for m in range(count):
        copy = pltpu.make_async_copy(own[m], full_ref.at[(m,) + pos], local_sem.at[m])
        copy.start()
        local.append(copy)
    for copy in cache_copies:
        copy.start()
    for copy in local:
        copy.wait()
    begin(count - 1, 1)

    def weight(m):
        held = full_ref[m]
        return held.reshape(math.prod(held.shape[:-1]), held.shape[-1])

    def straight(left, m):
        return jnp.dot(left, weight(m), preferred_element_type=jnp.float32)

    def exchange(index, values):
        swap_out[index] = values
        copy = pltpu.make_async_remote_copy(
            src_ref=swap_out.at[index],
            dst_ref=swap_in.at[index],
            send_sem=swap_send.at[index],
            recv_sem=swap_recv.at[index],
            device_id={"mp": 1 - mp},
            device_id_type=MESH,
        )
        copy.start()
        copy.wait()
        return values.astype(jnp.float32) + swap_in[index].astype(jnp.float32)

    def attend():
        normed = rms_scale(x_ref[...].astype(jnp.float32), attn_gain_ref[...])
        normed = normed.astype(jnp.bfloat16)
        query = straight(normed, 0) * scale_ref[...] / math.sqrt(head_size)
        query_buf[...] = query.astype(jnp.bfloat16)
        fresh_buf[0] = straight(normed, 1).astype(jnp.bfloat16)
        fresh_buf[1] = straight(normed, 2).astype(jnp.bfloat16)
        for copy in cache_copies:
            copy.wait()
        rows = spread_ref.shape[1]
        slots = spread_ref.shape[0]
        context_len = slots // rows

        def to_heads(product):
            high = product.astype(jnp.bfloat16)
            low = (product - high.astype(jnp.float32)).astype(jnp.bfloat16)
            return dot_t(high, heads_ref[...]) + dot_t(low, heads_ref[...])

        def from_heads(weights):
            return jnp.dot(weights, heads_ref[...], preferred_element_type=jnp.float32)

        def chunk(i, carry):
            at = pl.ds(pl.multiple_of(i * rows, rows), rows)
            wide = pl.ds(pl.multiple_of(i * slots, slots), slots)
            query = query_buf[at, :]
            spread = spread_ref[...]
            query_rep = jnp.dot(spread, query, preferred_element_type=jnp.float32)
            scores = to_heads(query_rep * key_buf[wide, :].astype(jnp.float32))
            own_score = to_heads(
                query.astype(jnp.float32) * fresh_buf[0, at, :].astype(jnp.float32)
            )
            limit = jnp.dot(spread, valid_ref[at, :], preferred_element_type=jnp.float32)
            lanes = scores.shape[1]
            scores = scores.reshape(rows, context_len, lanes)
            place = lax.broadcasted_iota(jnp.int32, scores.shape, 1).astype(jnp.float32)
            scores = jnp.where(place < limit.reshape(scores.shape), scores, -jnp.inf)
            highest = jnp.maximum(jnp.max(scores, axis=1), own_score)
            exp_cache = jnp.exp(scores - highest[:, None, :])
            exp_own = jnp.exp(own_score - highest)
            total = jnp.sum(exp_cache, axis=1) + exp_own
            weight_cache = (exp_cache / total[:, None, :]).astype(jnp.bfloat16)
            weight_own = (exp_own / total).astype(jnp.bfloat16)
            mixed = from_heads(weight_cache.reshape(slots, lanes))
            mixed = mixed * value_buf[wide, :].astype(jnp.float32)
            mixed = jnp.sum(mixed.reshape(rows, context_len, mixed.shape[1]), axis=1)
            mixed = mixed + from_heads(weight_own) * fresh_buf[1, at, :].astype(jnp.float32)
            context_buf[at, :] = mixed.astype(jnp.bfloat16)
            return carry

        lax.fori_loop(0, query_buf.shape[0] // rows, chunk, 0)

    for m in range(count - 1):
        begin(m, 1)
        if m + ahead < count - 1:
            begin(m + ahead, 0)
        if m >= 1:
            begin(m - 1, 2)
        if m == 5:
            begin(count - 1, 2)
            for k in range(3):
                arrive(k)
            attend()
    begin(count - 2, 2)
    arrive(3)
    stream1 = x_ref[...].astype(jnp.float32) + exchange(
        0, dot_t(context_buf[...], weight(3)).astype(jnp.bfloat16)
    )
    normed2 = rms_scale(stream1, mlp_gain_ref[...]).astype(jnp.bfloat16)
    arrive(4)
    hidden = jnp.maximum(straight(normed2, 4), 0.0).astype(jnp.bfloat16)
    arrive(5)
    stream2 = stream1 + exchange(1, dot_t(hidden, weight(5)).astype(jnp.bfloat16))
    stream2 = stream2.astype(jnp.bfloat16)
    half = half_bf.shape[2]
    half_bf[0] = stream2[:, :half]
    half_bf[1] = stream2[:, half:]
    arrive(6)
    head_pre = straight(stream2, 6)
    head_act = (head_pre / (1.0 + jnp.exp(-head_pre))).astype(jnp.bfloat16)
    arrive(8)
    skip = dot_t(half_bf[mp], weight(8))
    arrive(7)
    levels = dot_t(head_act, weight(7)) + skip
    width = half_f32.shape[2]
    for k in range(2):
        part = levels[:, k * width : (k + 1) * width]
        half_f32[k] = part
        part_bf[k] = part.astype(jnp.bfloat16)
    copy = pltpu.make_async_remote_copy(
        src_ref=part_bf.at[1 - mp],
        dst_ref=part_in,
        send_sem=swap_send.at[2],
        recv_sem=swap_recv.at[2],
        device_id={"mp": 1 - mp},
        device_id_type=MESH,
    )
    copy.start()
    copy.wait()
    out_ref[...] = half_f32[mp] + part_in[...].astype(jnp.float32)
    for copy in sent:
        copy.wait_send()


def fused_block(sizes, *args):
    x, keys, values, valid, attn_gain, mlp_gain, query_scale = args[:7]
    w_qkv, w_out, w_up, w_down, head_hidden, final = args[7:]
    rows, context_len, width = keys.shape
    features = x.shape[1]
    head_size = query_scale.shape[0]
    lanes = 128
    group = 16
    valid_lanes = jnp.broadcast_to(valid.astype(jnp.bfloat16)[:, None], (rows, lanes))
    spread = (jnp.arange(group * context_len)[:, None] // context_len == jnp.arange(group)).astype(
        jnp.bfloat16
    )
    heads = (jnp.arange(lanes)[:, None] == jnp.arange(width) // head_size).astype(jnp.bfloat16)
    scale = jnp.tile(query_scale, width // head_size)[None]
    slots = sum(size - 1 for size in sizes)
    own_rows = w_up.shape[0]
    out_width = final.shape[2] * math.prod(sizes) // 2
    vmem = pl.BlockSpec(memory_space=pltpu.VMEM)
    hbm = pl.BlockSpec(memory_space=pl.ANY)
    bf16, f32 = jnp.bfloat16, jnp.float32
    return pl.pallas_call(
        functools.partial(block_kernel, sizes, head_size),
        out_shape=jax.ShapeDtypeStruct((rows, out_width), f32),
        in_specs=[vmem, hbm, hbm] + [vmem] * 12,
        out_specs=vmem,
        scratch_shapes=[
            pltpu.VMEM((9,) + sizes + (own_rows, width), bf16),
            pltpu.VMEM((rows * context_len, width), bf16),
            pltpu.VMEM((rows * context_len, width), bf16),
            pltpu.VMEM((rows, width), bf16),
            pltpu.VMEM((2, rows, width), bf16),
            pltpu.VMEM((rows, width), bf16),
            pltpu.VMEM((2, rows, features), bf16),
            pltpu.VMEM((2, rows, features), bf16),
            pltpu.VMEM((2, rows, features // 2), bf16),
            pltpu.VMEM((2, rows, out_width), f32),
            pltpu.VMEM((2, rows, out_width), bf16),
            pltpu.VMEM((rows, out_width), bf16),
            pltpu.SemaphoreType.DMA((2,)),
            pltpu.SemaphoreType.DMA((9,)),
            pltpu.SemaphoreType.DMA((9, slots)),
            pltpu.SemaphoreType.DMA((9, slots)),
            pltpu.SemaphoreType.DMA((3,)),
            pltpu.SemaphoreType.DMA((3,)),
        ],
        compiler_params=pltpu.CompilerParams(
            collective_id=0, has_side_effects=True, vmem_limit_bytes=58 * 1024 * 1024
        ),
        name="decode_block",
    )(
        x,
        keys.reshape(rows * context_len, width),
        values.reshape(rows * context_len, width),
        valid_lanes,
        attn_gain[None],
        mlp_gain[None],
        scale,
        spread,
        heads,
        w_qkv,
        w_out.T,
        w_up,
        w_down.T,
        head_hidden,
        jnp.swapaxes(final, 1, 2),
    )


def gather_all(owns):
    return lax.all_gather(jnp.concatenate(owns, axis=0), "dp", axis=1, tiled=True)


def swap(values):
    return lax.ppermute(values, "mp", [(0, 1), (1, 0)])


def rms_scale(values, gain):
    meansq = jnp.mean(values * values, axis=-1, keepdims=True)
    return values * lax.rsqrt(meansq + 1e-06) * gain


def dot_t(left, right):
    return lax.dot_general(
        left, right, (((1,), (1,)), ((), ())), preferred_element_type=jnp.float32
    )


def per_device(
    sizes,
    new_embed,
    context_key_cache,
    value_cache,
    valid,
    attn_gain,
    mlp_gain,
    query_scale,
    w_qkv,
    w_out,
    w_up,
    w_down,
    head_hidden,
    final_layer_matrices,
):
    if w_up.shape[0] % 16 == 0:
        return fused_block(
            sizes,
            new_embed,
            context_key_cache,
            value_cache,
            valid,
            attn_gain,
            mlp_gain,
            query_scale,
            w_qkv,
            w_out,
            w_up,
            w_down,
            head_hidden,
            final_layer_matrices,
        )
    row_count = new_embed.shape[0]
    context_len = context_key_cache.shape[1]
    local_width = context_key_cache.shape[2]
    head_size = query_scale.shape[0]
    local_heads = local_width // head_size
    mp_index = lax.axis_index("mp")
    owns = [
        w_qkv,
        w_out.T[None],
        w_up[None],
        w_down.T[None],
        head_hidden[None],
        jnp.swapaxes(final_layer_matrices, 1, 2),
    ]
    full = gather_all(owns)
    stream = new_embed.astype(jnp.float32)
    normed = rms_scale(stream, attn_gain).astype(jnp.bfloat16)
    projected = [jnp.dot(normed, full[j], preferred_element_type=jnp.float32) for j in range(3)]
    query_all = projected[0].reshape(row_count, local_heads, head_size)
    query_all = (query_all * query_scale / math.sqrt(head_size)).astype(jnp.bfloat16)
    key_new = projected[1].astype(jnp.bfloat16).reshape(row_count, local_heads, head_size)
    value_new = projected[2].astype(jnp.bfloat16).reshape(row_count, local_heads, head_size)
    cache_keys = context_key_cache.reshape(row_count, context_len, local_heads, head_size)
    cache_vals = value_cache.reshape(row_count, context_len, local_heads, head_size)
    scores = jnp.einsum("bhe,bche->bhc", query_all, cache_keys, preferred_element_type=jnp.float32)
    own_score = jnp.sum(query_all.astype(jnp.float32) * key_new.astype(jnp.float32), axis=-1)
    in_use = jnp.arange(context_len, dtype=jnp.int32)[None, :] < valid[:, None]
    scores = jnp.where(in_use[:, None, :], scores, -jnp.inf)
    highest = jnp.maximum(jnp.max(scores, axis=-1), own_score)
    exp_cache = jnp.exp(scores - highest[..., None])
    exp_own = jnp.exp(own_score - highest)
    denominator = jnp.sum(exp_cache, axis=-1) + exp_own
    weight_cache = (exp_cache / denominator[..., None]).astype(jnp.bfloat16)
    weight_own = (exp_own / denominator).astype(jnp.bfloat16)
    context = jnp.einsum(
        "bhc,bche->bhe", weight_cache, cache_vals, preferred_element_type=jnp.float32
    )
    context = context + weight_own.astype(jnp.float32)[..., None] * value_new.astype(jnp.float32)
    context = context.astype(jnp.bfloat16).reshape(row_count, local_width)
    attention = dot_t(context, full[3]).astype(jnp.bfloat16)
    stream1 = stream + (attention.astype(jnp.float32) + swap(attention).astype(jnp.float32))
    normed2 = rms_scale(stream1, mlp_gain).astype(jnp.bfloat16)
    up_act = jnp.dot(normed2, full[4], preferred_element_type=jnp.float32)
    hidden = jax.nn.relu(up_act).astype(jnp.bfloat16)
    feed_out = dot_t(hidden, full[5]).astype(jnp.bfloat16)
    stream2 = stream1 + (feed_out.astype(jnp.float32) + swap(feed_out).astype(jnp.float32))
    stream2 = stream2.astype(jnp.bfloat16)
    half = final_layer_matrices.shape[1]
    stream_half = lax.dynamic_slice_in_dim(stream2, mp_index * half, half, 1)
    head_pre = jnp.dot(stream2, full[6], preferred_element_type=jnp.float32)
    head_act = jax.nn.silu(head_pre).astype(jnp.bfloat16)
    partial_out = dot_t(head_act, full[7]) + dot_t(stream_half, full[8])
    out_half = partial_out.shape[1] // 2
    mine = lax.dynamic_slice_in_dim(partial_out, mp_index * out_half, out_half, 1)
    theirs = lax.dynamic_slice_in_dim(partial_out, (1 - mp_index) * out_half, out_half, 1)
    return mine + swap(theirs.astype(jnp.bfloat16)).astype(jnp.float32)


def solution(mesh):
    in_specs = (
        P("dp", None),
        P("dp", None, "mp"),
        P("dp", None, "mp"),
        P("dp"),
        P(),
        P(),
        P(),
        P(None, "dp", "mp"),
        P("mp", "dp"),
        P("dp", "mp"),
        P("mp", "dp"),
        P("dp", "mp"),
        P(None, "mp", "dp"),
    )
    out_specs = P("dp", "mp")
    return jax.shard_map(
        functools.partial(per_device, grid_of(mesh)),
        mesh=mesh,
        in_specs=in_specs,
        out_specs=out_specs,
        check_vma=False,
    )
```

```python
import functools
import math

import jax
import jax.numpy as jnp
from jax import lax
from jax.experimental import pallas as pl
from jax.experimental.pallas import tpu as pltpu
from jax.sharding import PartitionSpec as P

MESH = pl.DeviceIdType.MESH


def grid_of(mesh):
    count = mesh.shape["dp"]
    try:
        coords = [tuple(d.coords) for d in mesh.devices[:, 0]]
        sizes = [len({c[k] for c in coords}) for k in (2, 1, 0)]
    except Exception:
        sizes = [count, 1, 1]
    if math.prod(sizes) != count:
        sizes = [count, 1, 1]
    return tuple(sizes)


def axis_orders(count):
    pattern = ((0, 1, 2), (0, 2, 1), (0, 1, 2), (0, 2, 1), (0, 1, 2), (0, 2, 1), (0, 1, 2), (2, 1, 0), (1, 2, 0))
    return [pattern[m % len(pattern)] for m in range(count)]


def block_kernel(
    sizes,
    head_size,
    x_ref,
    key_ref,
    value_ref,
    valid_ref,
    attn_gain_ref,
    mlp_gain_ref,
    scale_ref,
    spread_ref,
    heads_ref,
    w_qkv_ref,
    w_out_ref,
    w_up_ref,
    w_down_ref,
    head_ref,
    final_ref,
    out_ref,
    full_ref,
    key_buf,
    value_buf,
    query_buf,
    fresh_buf,
    context_buf,
    swap_out,
    swap_in,
    half_bf,
    half_f32,
    part_bf,
    part_in,
    cache_sem,
    local_sem,
    send_sem,
    recv_sem,
    swap_send,
    swap_recv,
):
    own = [w_qkv_ref.at[j] for j in range(3)]
    own += [w_out_ref, w_up_ref, w_down_ref, head_ref, final_ref.at[0], final_ref.at[1]]
    count = len(own)
    orders = axis_orders(count)
    me = lax.axis_index("dp")
    mp = lax.axis_index("mp")
    spans = (sizes[1] * sizes[2], sizes[2], 1)
    pos = tuple((me // spans[k]) % sizes[k] for k in range(3))

    def peer(axis, step):
        other = lax.rem(pos[axis] + step, sizes[axis])
        return me + (other - pos[axis]) * spans[axis]

    cache_copies = [
        pltpu.make_async_copy(key_ref, key_buf, cache_sem.at[0]),
        pltpu.make_async_copy(value_ref, value_buf, cache_sem.at[1]),
    ]
    barrier = pltpu.get_barrier_semaphore()
    peers = [(axis, step) for axis in range(3) for step in range(1, sizes[axis])]
    for axis, step in peers:
        pl.semaphore_signal(barrier, inc=1, device_id={"dp": peer(axis, step)}, device_id_type=MESH)
    pl.semaphore_signal(barrier, inc=1, device_id={"mp": 1 - mp}, device_id_type=MESH)
    pl.semaphore_wait(barrier, len(peers) + 1)
    slot = {key: i for i, key in enumerate(peers)}

    def copies(m, phase):
        axis = orders[m][phase]
        done = orders[m][:phase]
        target = full_ref.at[(m,) + tuple(slice(None) if k in done else pos[k] for k in range(3))]
        return [
            pltpu.make_async_remote_copy(
                src_ref=target if phase else own[m],
                dst_ref=target,
                send_sem=send_sem.at[m, slot[axis, step]],
                recv_sem=recv_sem.at[m, slot[axis, step]],
                device_id={"dp": peer(axis, step)},
                device_id_type=MESH,
            )
            for step in range(1, sizes[axis])
        ]

    flying = [None] * count
    sent = []

    def arrive(m):
        for copy in flying[m]:
            copy.wait_recv()
        sent.extend(flying[m])

    def begin(m, phase):
        if phase:
            arrive(m)
        flying[m] = copies(m, phase)
        for copy in flying[m]:
            copy.start()

    ahead = 3
    plain = count - 2
    for m in [0] + list(range(plain, count)) + list(range(1, ahead)):
        begin(m, 0)
    local = []
    for m in range(count):
        copy = pltpu.make_async_copy(own[m], full_ref.at[(m,) + pos], local_sem.at[m])
        copy.start()
        local.append(copy)
    for copy in cache_copies:
        copy.start()
    for copy in local:
        copy.wait()
    for m in range(plain, count):
        begin(m, 1)

    def weight(m):
        held = full_ref[m]
        return held.reshape(math.prod(held.shape[:-1]), held.shape[-1])

    def straight(left, m):
        return jnp.dot(left, weight(m), preferred_element_type=jnp.float32)

    def exchange(index, values):
        swap_out[index] = values
        copy = pltpu.make_async_remote_copy(
            src_ref=swap_out.at[index],
            dst_ref=swap_in.at[index],
            send_sem=swap_send.at[index],
            recv_sem=swap_recv.at[index],
            device_id={"mp": 1 - mp},
            device_id_type=MESH,
        )
        copy.start()
        copy.wait()
        return values.astype(jnp.float32) + swap_in[index].astype(jnp.float32)

    def attend():
        normed = rms_scale(x_ref[...].astype(jnp.float32), attn_gain_ref[...])
        normed = normed.astype(jnp.bfloat16)
        query = straight(normed, 0) * scale_ref[...] / math.sqrt(head_size)
        query_buf[...] = query.astype(jnp.bfloat16)
        fresh_buf[0] = straight(normed, 1).astype(jnp.bfloat16)
        fresh_buf[1] = straight(normed, 2).astype(jnp.bfloat16)
        for copy in cache_copies:
            copy.wait()
        rows = spread_ref.shape[1]
        slots = spread_ref.shape[0]
        context_len = slots // rows

        def to_heads(product):
            high = product.astype(jnp.bfloat16)
            low = (product - high.astype(jnp.float32)).astype(jnp.bfloat16)
            return dot_t(high, heads_ref[...]) + dot_t(low, heads_ref[...])

        def from_heads(weights):
            return jnp.dot(weights, heads_ref[...], preferred_element_type=jnp.float32)

        def chunk(i, carry):
            at = pl.ds(pl.multiple_of(i * rows, rows), rows)
            wide = pl.ds(pl.multiple_of(i * slots, slots), slots)
            query = query_buf[at, :]
            spread = spread_ref[...]
            query_rep = jnp.dot(spread, query, preferred_element_type=jnp.float32)
            scores = to_heads(query_rep * key_buf[wide, :].astype(jnp.float32))
            own_score = to_heads(
                query.astype(jnp.float32) * fresh_buf[0, at, :].astype(jnp.float32)
            )
            limit = jnp.dot(spread, valid_ref[at, :], preferred_element_type=jnp.float32)
            lanes = scores.shape[1]
            scores = scores.reshape(rows, context_len, lanes)
            place = lax.broadcasted_iota(jnp.int32, scores.shape, 1).astype(jnp.float32)
            scores = jnp.where(place < limit.reshape(scores.shape), scores, -jnp.inf)
            highest = jnp.maximum(jnp.max(scores, axis=1), own_score)
            exp_cache = jnp.exp(scores - highest[:, None, :])
            exp_own = jnp.exp(own_score - highest)
            total = jnp.sum(exp_cache, axis=1) + exp_own
            weight_cache = (exp_cache / total[:, None, :]).astype(jnp.bfloat16)
            weight_own = (exp_own / total).astype(jnp.bfloat16)
            mixed = from_heads(weight_cache.reshape(slots, lanes))
            mixed = mixed * value_buf[wide, :].astype(jnp.float32)
            mixed = jnp.sum(mixed.reshape(rows, context_len, mixed.shape[1]), axis=1)
            mixed = mixed + from_heads(weight_own) * fresh_buf[1, at, :].astype(jnp.float32)
            context_buf[at, :] = mixed.astype(jnp.bfloat16)
            return carry

        lax.fori_loop(0, query_buf.shape[0] // rows, chunk, 0)

    for m in range(plain):
        begin(m, 1)
        if m + ahead < plain:
            begin(m + ahead, 0)
        if m >= 1:
            begin(m - 1, 2)
        if m == 3:
            for k in range(plain, count):
                begin(k, 2)
        if m == 5:
            for k in range(3):
                arrive(k)
            attend()
    begin(plain - 1, 2)
    arrive(3)
    stream1 = x_ref[...].astype(jnp.float32) + exchange(
        0, dot_t(context_buf[...], weight(3)).astype(jnp.bfloat16)
    )
    normed2 = rms_scale(stream1, mlp_gain_ref[...]).astype(jnp.bfloat16)
    arrive(4)
    hidden = jnp.maximum(straight(normed2, 4), 0.0).astype(jnp.bfloat16)
    arrive(5)
    stream2 = stream1 + exchange(1, dot_t(hidden, weight(5)).astype(jnp.bfloat16))
    stream2 = stream2.astype(jnp.bfloat16)
    half = half_bf.shape[2]
    half_bf[0] = stream2[:, :half]
    half_bf[1] = stream2[:, half:]
    arrive(6)
    head_pre = straight(stream2, 6)
    head_act = (head_pre / (1.0 + jnp.exp(-head_pre))).astype(jnp.bfloat16)
    arrive(8)
    skip = dot_t(half_bf[mp], weight(8))
    arrive(7)
    levels = dot_t(head_act, weight(7)) + skip
    width = half_f32.shape[2]
    for k in range(2):
        part = levels[:, k * width : (k + 1) * width]
        half_f32[k] = part
        part_bf[k] = part.astype(jnp.bfloat16)
    copy = pltpu.make_async_remote_copy(
        src_ref=part_bf.at[1 - mp],
        dst_ref=part_in,
        send_sem=swap_send.at[2],
        recv_sem=swap_recv.at[2],
        device_id={"mp": 1 - mp},
        device_id_type=MESH,
    )
    copy.start()
    copy.wait()
    out_ref[...] = half_f32[mp] + part_in[...].astype(jnp.float32)
    for copy in sent:
        copy.wait_send()


def fused_block(sizes, *args):
    x, keys, values, valid, attn_gain, mlp_gain, query_scale = args[:7]
    w_qkv, w_out, w_up, w_down, head_hidden, final = args[7:]
    rows, context_len, width = keys.shape
    features = x.shape[1]
    head_size = query_scale.shape[0]
    lanes = 128
    group = 16
    valid_lanes = jnp.broadcast_to(valid.astype(jnp.bfloat16)[:, None], (rows, lanes))
    spread = (jnp.arange(group * context_len)[:, None] // context_len == jnp.arange(group)).astype(
        jnp.bfloat16
    )
    heads = (jnp.arange(lanes)[:, None] == jnp.arange(width) // head_size).astype(jnp.bfloat16)
    scale = jnp.tile(query_scale, width // head_size)[None]
    slots = sum(size - 1 for size in sizes)
    own_rows = w_up.shape[0]
    out_width = final.shape[2] * math.prod(sizes) // 2
    vmem = pl.BlockSpec(memory_space=pltpu.VMEM)
    hbm = pl.BlockSpec(memory_space=pl.ANY)
    bf16, f32 = jnp.bfloat16, jnp.float32
    return pl.pallas_call(
        functools.partial(block_kernel, sizes, head_size),
        out_shape=jax.ShapeDtypeStruct((rows, out_width), f32),
        in_specs=[vmem, hbm, hbm] + [vmem] * 12,
        out_specs=vmem,
        scratch_shapes=[
            pltpu.VMEM((9,) + sizes + (own_rows, width), bf16),
            pltpu.VMEM((rows * context_len, width), bf16),
            pltpu.VMEM((rows * context_len, width), bf16),
            pltpu.VMEM((rows, width), bf16),
            pltpu.VMEM((2, rows, width), bf16),
            pltpu.VMEM((rows, width), bf16),
            pltpu.VMEM((2, rows, features), bf16),
            pltpu.VMEM((2, rows, features), bf16),
            pltpu.VMEM((2, rows, features // 2), bf16),
            pltpu.VMEM((2, rows, out_width), f32),
            pltpu.VMEM((2, rows, out_width), bf16),
            pltpu.VMEM((rows, out_width), bf16),
            pltpu.SemaphoreType.DMA((2,)),
            pltpu.SemaphoreType.DMA((9,)),
            pltpu.SemaphoreType.DMA((9, slots)),
            pltpu.SemaphoreType.DMA((9, slots)),
            pltpu.SemaphoreType.DMA((3,)),
            pltpu.SemaphoreType.DMA((3,)),
        ],
        compiler_params=pltpu.CompilerParams(
            collective_id=0, has_side_effects=True, vmem_limit_bytes=58 * 1024 * 1024
        ),
        name="decode_block",
    )(
        x,
        keys.reshape(rows * context_len, width),
        values.reshape(rows * context_len, width),
        valid_lanes,
        attn_gain[None],
        mlp_gain[None],
        scale,
        spread,
        heads,
        w_qkv,
        w_out.T,
        w_up,
        w_down.T,
        head_hidden,
        jnp.swapaxes(final, 1, 2),
    )


def gather_all(owns):
    return lax.all_gather(jnp.concatenate(owns, axis=0), "dp", axis=1, tiled=True)


def swap(values):
    return lax.ppermute(values, "mp", [(0, 1), (1, 0)])


def rms_scale(values, gain):
    meansq = jnp.mean(values * values, axis=-1, keepdims=True)
    return values * lax.rsqrt(meansq + 1e-06) * gain


def dot_t(left, right):
    return lax.dot_general(
        left, right, (((1,), (1,)), ((), ())), preferred_element_type=jnp.float32
    )


def per_device(
    sizes,
    new_embed,
    context_key_cache,
    value_cache,
    valid,
    attn_gain,
    mlp_gain,
    query_scale,
    w_qkv,
    w_out,
    w_up,
    w_down,
    head_hidden,
    final_layer_matrices,
):
    if w_up.shape[0] % 16 == 0:
        return fused_block(
            sizes,
            new_embed,
            context_key_cache,
            value_cache,
            valid,
            attn_gain,
            mlp_gain,
            query_scale,
            w_qkv,
            w_out,
            w_up,
            w_down,
            head_hidden,
            final_layer_matrices,
        )
    row_count = new_embed.shape[0]
    context_len = context_key_cache.shape[1]
    local_width = context_key_cache.shape[2]
    head_size = query_scale.shape[0]
    local_heads = local_width // head_size
    mp_index = lax.axis_index("mp")
    owns = [
        w_qkv,
        w_out.T[None],
        w_up[None],
        w_down.T[None],
        head_hidden[None],
        jnp.swapaxes(final_layer_matrices, 1, 2),
    ]
    full = gather_all(owns)
    stream = new_embed.astype(jnp.float32)
    normed = rms_scale(stream, attn_gain).astype(jnp.bfloat16)
    projected = [jnp.dot(normed, full[j], preferred_element_type=jnp.float32) for j in range(3)]
    query_all = projected[0].reshape(row_count, local_heads, head_size)
    query_all = (query_all * query_scale / math.sqrt(head_size)).astype(jnp.bfloat16)
    key_new = projected[1].astype(jnp.bfloat16).reshape(row_count, local_heads, head_size)
    value_new = projected[2].astype(jnp.bfloat16).reshape(row_count, local_heads, head_size)
    cache_keys = context_key_cache.reshape(row_count, context_len, local_heads, head_size)
    cache_vals = value_cache.reshape(row_count, context_len, local_heads, head_size)
    scores = jnp.einsum("bhe,bche->bhc", query_all, cache_keys, preferred_element_type=jnp.float32)
    own_score = jnp.sum(query_all.astype(jnp.float32) * key_new.astype(jnp.float32), axis=-1)
    in_use = jnp.arange(context_len, dtype=jnp.int32)[None, :] < valid[:, None]
    scores = jnp.where(in_use[:, None, :], scores, -jnp.inf)
    highest = jnp.maximum(jnp.max(scores, axis=-1), own_score)
    exp_cache = jnp.exp(scores - highest[..., None])
    exp_own = jnp.exp(own_score - highest)
    denominator = jnp.sum(exp_cache, axis=-1) + exp_own
    weight_cache = (exp_cache / denominator[..., None]).astype(jnp.bfloat16)
    weight_own = (exp_own / denominator).astype(jnp.bfloat16)
    context = jnp.einsum(
        "bhc,bche->bhe", weight_cache, cache_vals, preferred_element_type=jnp.float32
    )
    context = context + weight_own.astype(jnp.float32)[..., None] * value_new.astype(jnp.float32)
    context = context.astype(jnp.bfloat16).reshape(row_count, local_width)
    attention = dot_t(context, full[3]).astype(jnp.bfloat16)
    stream1 = stream + (attention.astype(jnp.float32) + swap(attention).astype(jnp.float32))
    normed2 = rms_scale(stream1, mlp_gain).astype(jnp.bfloat16)
    up_act = jnp.dot(normed2, full[4], preferred_element_type=jnp.float32)
    hidden = jax.nn.relu(up_act).astype(jnp.bfloat16)
    feed_out = dot_t(hidden, full[5]).astype(jnp.bfloat16)
    stream2 = stream1 + (feed_out.astype(jnp.float32) + swap(feed_out).astype(jnp.float32))
    stream2 = stream2.astype(jnp.bfloat16)
    half = final_layer_matrices.shape[1]
    stream_half = lax.dynamic_slice_in_dim(stream2, mp_index * half, half, 1)
    head_pre = jnp.dot(stream2, full[6], preferred_element_type=jnp.float32)
    head_act = jax.nn.silu(head_pre).astype(jnp.bfloat16)
    partial_out = dot_t(head_act, full[7]) + dot_t(stream_half, full[8])
    out_half = partial_out.shape[1] // 2
    mine = lax.dynamic_slice_in_dim(partial_out, mp_index * out_half, out_half, 1)
    theirs = lax.dynamic_slice_in_dim(partial_out, (1 - mp_index) * out_half, out_half, 1)
    return mine + swap(theirs.astype(jnp.bfloat16)).astype(jnp.float32)


def solution(mesh):
    in_specs = (
        P("dp", None),
        P("dp", None, "mp"),
        P("dp", None, "mp"),
        P("dp"),
        P(),
        P(),
        P(),
        P(None, "dp", "mp"),
        P("mp", "dp"),
        P("dp", "mp"),
        P("mp", "dp"),
        P("dp", "mp"),
        P(None, "mp", "dp"),
    )
    out_specs = P("dp", "mp")
    return jax.shard_map(
        functools.partial(per_device, grid_of(mesh)),
        mesh=mesh,
        in_specs=in_specs,
        out_specs=out_specs,
        check_vma=False,
    )
```
